32 devices in a mesh: mem: 2 (over y), space: 16 (over z, x, core).
Axes of the slice: x: 2, y: 2, z: 4, core: 2. Of those that a mesh axis runs over, the one named last changes fastest.
Arguments:
- ensemble: bfloat16 [64, 160, 32, 128], P('mem', None, 'space'), may hold values from -6 to 6
- obs_value: float32 [16, 256], P('space'), may hold values from -6 to 6
- obs_error: float32 [16, 256], P('space'), may hold values from 0.3 to 3
- obs_cell: int32 [16, 256], P('space'), may hold values from 0 to 255
- obs_species: int32 [16, 256], P('space'), may hold values from 0 to 39
- patch_index: int32 [16, 256, 32], P('space', 'mem'), may hold values from 0 to 767, as said below
- patch_count: int32 [16, 256], P('space', 'mem'), may hold values from 1 to 32, as said below
- courant_x: float32 [4, 32, 128], P(None, 'space'), may hold values from -0.7 to 0.7
- courant_y: float32 [4, 32, 128], P(None, 'space'), may hold values from -0.7 to 0.7
- dep_velocity: float32 [40], replicated, may hold values from 0.05 to 0.5
- surface_factor: float32 [32, 128], P('space'), may hold values from 0.5 to 2
Outputs:
- forecast: bfloat16 [64, 160, 32, 128], P('mem', None, 'space')
The draws below stay inside these ranges and needn't reach their ends.
Inputs may be any that keep to these rules, and one draw needn't show every extreme that they name: `patch_index`: each cell's list names distinct pool observations of existing tiles, nearest to the cell first; those within 3 cells of the cell come first. `patch_count`: the number of listed observations used for the cell, at least 1 and at most 32; the most is reached in every draw.
All inputs are finite; a program needn't handle non-finite values.
Results may differ from the reference program's by a relative error of at most 0.0049.
Values may be sent and summed in bfloat16 or wider, within the bound.
A program may use at most 64 MiB of HBM per device.

```python
import math
import jax
import jax.numpy as jnp
from jax import lax

MEMBERS = 64
SPECIES = 40
LEVELS = 4
NX = 128
ROWS = 2
OBS_TILE = 256
MAXOBS = 32
NEWTON = 8
SUBSTEPS = 2
TILES = 16
NY = 32
FIELDS = 160
LOC = 1


def shared_cells(key):
    return jax.random.randint(jax.random.fold_in(key, 7177), (TILES, OBS_TILE), 0, ROWS * NX, dtype=jnp.int32)


def nearest_lists(key):
    cells = shared_cells(key)
    padded = jnp.pad(cells, ((1, 1), (0, 0)))
    tile_ids = jnp.arange(TILES, dtype=jnp.int32)
    reach = 3 * LOC

    def one_tile(tile_num):
        pool_cells = lax.dynamic_slice_in_dim(padded, tile_num, 3, 0)
        offsets = (jnp.arange(3, dtype=jnp.int32) - 1) * ROWS
        pool_row = (pool_cells // NX + offsets[:, None]).reshape(-1)
        pool_col = (pool_cells % NX).reshape(-1)
        source_tile = tile_num - 1 + jnp.arange(3, dtype=jnp.int32)
        exists = (source_tile >= 0) & (source_tile < TILES)
        exists = jnp.broadcast_to(exists[:, None], (3, OBS_TILE)).reshape(-1)
        cell_ids = jnp.arange(ROWS * NX, dtype=jnp.int32)
        cell_row = cell_ids // NX
        cell_col = cell_ids % NX
        dist_sq = (pool_row[None, :] - cell_row[:, None]) ** 2 + (pool_col[None, :] - cell_col[:, None]) ** 2
        dist_sq = jnp.where(exists[None, :], dist_sq, 40000)
        score = dist_sq * 2048 + jnp.arange(3 * OBS_TILE, dtype=jnp.int32)[None, :]
        neg_top, chosen = lax.top_k(-score, MAXOBS)
        near = jnp.sum(((dist_sq <= reach * reach) & exists[None, :]).astype(jnp.int32), axis=1)
        return (chosen.astype(jnp.int32), jnp.clip(near, 1, MAXOBS).astype(jnp.int32))
    chosen, counts = lax.map(one_tile, tile_ids)
    counts = counts.at[0, 0].set(MAXOBS)
    return (chosen, counts)


def draw_obs_cell(key, part):
    return shared_cells(key)


def draw_patch_index(key, part):
    return nearest_lists(key)[0]


def draw_patch_count(key, part):
    return nearest_lists(key)[1]


def touch_ends(array, stream_key, smallest, largest):
    longest = array.shape.index(max(array.shape))
    spots = []
    for shift in (0, 1):
        where = [jax.random.randint(jax.random.fold_in(stream_key, axis), (), 0, length) for axis, length in enumerate(array.shape)]
        where[longest] = (where[longest] + shift) % array.shape[longest]
        spots.append(tuple(where))
    return array.at[spots[0]].set(smallest).at[spots[1]].set(largest)


def block_levels(stream_key, dims, split, least, largest):
    def one(axis_at, parts):
        draws = jax.random.uniform(jax.random.fold_in(jax.random.fold_in(stream_key, 6), axis_at), (parts,), jnp.float32, least / len(split), largest / len(split))
        return jnp.repeat(jnp.exp(draws), dims[axis_at] // parts).reshape((-1,) + (1,) * (len(dims) - axis_at - 1))

    level = one(*split[0])
    for cut in split[1:]:
        level = level * one(*cut)
    return level


def noise(stream_key, extent, spread, most, pieces=(), kind=jnp.bfloat16):
    array = jax.random.normal(stream_key, extent, jnp.float32) * spread
    if len(pieces) > 0:
        array = block_levels(stream_key, extent, pieces, -0.22, 0.18) * array
    return jnp.clip(array, min=-most, max=most).astype(kind)


def setup_inputs(seed: int = 0) -> dict:
    splits = jax.random.split(jax.random.key(seed), 12)
    return {
        "ensemble": noise(splits[0], (MEMBERS, FIELDS, NY, NX), 1.0, 6.0, ((0, 2), (2, 16))),
        "obs_value": noise(splits[1], (TILES, OBS_TILE), 1.0, 6.0, ((0, 16),), jnp.float32),
        "obs_error": jnp.clip(jnp.exp(math.log(3.0) - 2.3025851 * jax.random.uniform(splits[2], (TILES, OBS_TILE), jnp.float32) ** block_levels(splits[2], (TILES, OBS_TILE), ((0, 16),), -0.2, 0.2)), 0.3, 3.0),
        "obs_cell": draw_obs_cell(jax.random.fold_in(splits[11], 71), 0),
        "obs_species": touch_ends(jax.random.randint(splits[4], (TILES, OBS_TILE), 0, SPECIES), jax.random.fold_in(splits[4], 1), 0, SPECIES - 1).astype(jnp.int32),
        "patch_index": draw_patch_index(jax.random.fold_in(splits[11], 71), 0),
        "patch_count": draw_patch_count(jax.random.fold_in(splits[11], 71), 0),
        "courant_x": jnp.clip(jax.random.uniform(splits[7], (LEVELS, NY, NX), jnp.float32, -0.7, 0.7) * block_levels(splits[7], (LEVELS, NY, NX), ((1, 16),), -0.4, 0.0), -0.7, 0.7),
        "courant_y": jnp.clip(jax.random.uniform(splits[8], (LEVELS, NY, NX), jnp.float32, -0.7, 0.7) * block_levels(splits[8], (LEVELS, NY, NX), ((1, 16),), -0.4, 0.0), -0.7, 0.7),
        "dep_velocity": jnp.clip(jnp.exp(jax.random.uniform(splits[9], (SPECIES,), jnp.float32, math.log(0.05), math.log(0.5))), 0.05, 0.5),
        "surface_factor": jnp.clip(0.5 + 1.5 * jax.random.uniform(splits[10], (NY, NX), jnp.float32) ** block_levels(splits[10], (NY, NX), ((0, 16),), -0.2, 0.2), 0.5, 2.0),
    }


def inverse_root(matrix, trace_val, repeats):
    matrix_order = matrix.shape[-1]
    identity = jnp.eye(matrix_order, dtype=jnp.float32)
    iterate = matrix / trace_val[:, None, None]
    inv_root = jnp.broadcast_to(identity, matrix.shape)
    for repeat in range(repeats):
        middle = 1.5 * identity - 0.5 * jnp.einsum('cij,cjk->cik', inv_root, iterate, precision=lax.Precision.HIGHEST)
        iterate = jnp.einsum('cij,cjk->cik', iterate, middle, precision=lax.Precision.HIGHEST)
        inv_root = jnp.einsum('cij,cjk->cik', middle, inv_root, precision=lax.Precision.HIGHEST)
    return inv_root

def prepare_pool(obs_pool, members, row_offsets):
    pooled = jnp.transpose(obs_pool[:, :members], (1, 0, 2)).reshape(members, -1)
    extra = obs_pool[:, members:]
    obs_mean = lax.optimization_barrier(jnp.mean(pooled, axis=0))
    obs_dev = jnp.transpose(pooled - obs_mean[None, :])
    values = extra[:, 0].reshape(-1)
    errors = extra[:, 1].reshape(-1)
    obs_row = (extra[:, 2] + row_offsets[:, None]).reshape(-1)
    obs_col = extra[:, 3].reshape(-1)
    return (obs_dev, obs_mean, values, errors, obs_row, obs_col)

def analyse(block_state, prepared, indices, counts, cell_ids, columns, radius, repeats):
    obs_dev, obs_mean, values, errors, obs_row, obs_col = prepared
    members = obs_dev.shape[1]
    picked = obs_dev[indices]
    cell_row = (cell_ids // columns).astype(jnp.float32)
    cell_col = (cell_ids % columns).astype(jnp.float32)
    distance_sq = (obs_row[indices] - cell_row[:, None]) ** 2 + (obs_col[indices] - cell_col[:, None]) ** 2
    active = jnp.arange(indices.shape[1], dtype=jnp.int32)[None, :] < counts[:, None]
    obs_weight = jnp.where(active, jnp.exp(-distance_sq / (2.0 * radius * radius)) / errors[indices], 0.0)
    innovation = values[indices] - obs_mean[indices]
    identity = jnp.eye(members, dtype=jnp.float32)
    gram_mat = jnp.einsum('cok,col->ckl', picked * obs_weight[:, :, None], picked, precision=lax.Precision.HIGHEST) + (members - 1.0) * identity
    trace_val = jnp.einsum('ckk->c', gram_mat)
    inv_root = inverse_root(gram_mat, trace_val, repeats)
    gain_vec = jnp.einsum('cok,co->ck', picked, obs_weight * innovation, precision=lax.Precision.HIGHEST)
    analysis_cov = jnp.einsum('ckl,clm->ckm', inv_root, inv_root, precision=lax.Precision.HIGHEST) / trace_val[:, None, None]
    mean_w = jnp.einsum('ckl,cl->ck', analysis_cov, gain_vec, precision=lax.Precision.HIGHEST)
    weights = math.sqrt(members - 1.0) * inv_root / jnp.sqrt(trace_val)[:, None, None] + mean_w[:, :, None]
    state_mean = lax.optimization_barrier(jnp.mean(block_state, axis=0))
    state_dev = block_state - state_mean[None]
    result = state_mean[None] + jnp.einsum('ifc,cij->jfc', state_dev, weights, precision=lax.Precision.HIGHEST)
    return result.astype(jnp.bfloat16)

def rows_step(extended, courant):
    middle = extended[..., 1:-1, :]
    north_row = extended[..., 2:, :]
    south_row = extended[..., :-2, :]
    return middle - 0.5 * courant * (north_row - south_row) + 0.5 * courant * courant * (north_row - 2.0 * middle + south_row)

def cols_step(field_now, courant):
    padded = jnp.pad(field_now, [(0, 0)] * (field_now.ndim - 1) + [(1, 1)])
    middle = padded[..., 1:-1]
    east_col = padded[..., 2:]
    west_col = padded[..., :-2]
    return middle - 0.5 * courant * (east_col - west_col) + 0.5 * courant * courant * (east_col - 2.0 * middle + west_col)

def deposit(field_now, dep_velocity, surface_factor):
    loss = jnp.exp(-dep_velocity[:, None, None] * surface_factor[None])
    lowest = (jnp.arange(field_now.shape[2], dtype=jnp.int32) == 0)[:, None, None]
    factor = jnp.where(lowest[None], loss[:, None], 1.0)
    return field_now * factor[None]

def reference(ensemble, obs_value, obs_error, obs_cell, obs_species, patch_index, patch_count, courant_x, courant_y, dep_velocity, surface_factor):
    tile_cells = ROWS * NX
    by_tile = jnp.transpose(ensemble.reshape(MEMBERS, FIELDS, TILES, tile_cells), (2, 0, 1, 3))
    flat_state = by_tile.reshape(TILES, MEMBERS, FIELDS * tile_cells)
    position = obs_species * (LEVELS * tile_cells) + obs_cell
    position = jnp.broadcast_to(position[:, None, :], (TILES, MEMBERS, OBS_TILE))
    equivalents = jnp.take_along_axis(flat_state, position, axis=2).astype(jnp.float32)
    obs_info = jnp.stack([obs_value, obs_error, (obs_cell // NX).astype(jnp.float32), (obs_cell % NX).astype(jnp.float32)], axis=1)
    packed = jnp.concatenate([equivalents, obs_info], axis=1)
    padded = jnp.pad(packed, ((1, 1), (0, 0), (0, 0)))
    row_offsets = (jnp.arange(3, dtype=jnp.float32) - 1.0) * ROWS

    def one_tile(tile_num):
        obs_pool = lax.dynamic_slice_in_dim(padded, tile_num, 3, 0)
        prepared = prepare_pool(obs_pool, MEMBERS, row_offsets)
        block_state = by_tile[tile_num].astype(jnp.float32)
        cell_ids = jnp.arange(tile_cells, dtype=jnp.int32)
        return analyse(block_state, prepared, patch_index[tile_num], patch_count[tile_num], cell_ids, NX, LOC, NEWTON)
    analysed = lax.map(one_tile, jnp.arange(TILES, dtype=jnp.int32))
    analysed = jnp.transpose(analysed, (1, 2, 0, 3)).reshape(MEMBERS, SPECIES, LEVELS, NY, NX)
    field_now = analysed.astype(jnp.float32)
    for repeat in range(SUBSTEPS):
        padded_rows = jnp.pad(field_now, ((0, 0), (0, 0), (0, 0), (1, 1), (0, 0)))
        field_now = rows_step(padded_rows, courant_y)
        field_now = cols_step(field_now, courant_x)
    field_now = deposit(field_now, dep_velocity, surface_factor)
    return field_now.reshape(MEMBERS, FIELDS, NY, NX).astype(jnp.bfloat16)
```

```python
import functools
import math

import jax
import jax.numpy as jnp
from jax import lax
from jax.experimental import pallas as pl
from jax.experimental.pallas import tpu as pltpu
from jax.sharding import PartitionSpec as P

NEWTON = 8
SUBSTEPS = 2
LOC = 1
LANES = 128
GROUP = 8
INTERPRET = False


def lane_product(left, right, depth, rows, width, finish, unroll=4):
    def group(block, carry):
        first = pl.multiple_of(block * GROUP, GROUP)

        def step(k, sums):
            row = right(k)
            return tuple(sums[r] + left(k, first, r) * row for r in range(GROUP))

        zero = jnp.zeros((width, LANES), jnp.float32)
        sums = lax.fori_loop(0, depth, step, (zero,) * GROUP, unroll=unroll)
        finish(first, sums)
        return carry

    lax.fori_loop(0, rows // GROUP, group, 0)


def weights_kernel(
    members, repeats, radius,
    pool_ref, idx_ref, cnt_ref, row_ref, col_ref,
    dev_ref, mix_ref, keep_ref,
    gram, prod, root, core, half, innov,
):
    slots = idx_ref.shape[0]
    pooled = pool_ref.shape[1]
    info = pool_ref[members:, :]
    high = info.astype(jnp.bfloat16).astype(jnp.float32)
    rest = info - high
    middle = rest.astype(jnp.bfloat16).astype(jnp.float32)
    low = rest - middle
    table = jnp.concatenate([pool_ref[:members, :], high, middle, low, jnp.zeros_like(low)], axis=0)
    table = table.astype(jnp.bfloat16)
    place = lax.broadcasted_iota(jnp.int32, (pooled, LANES), 0)
    extra = info.shape[0]

    def pick(k, total):
        hot = jnp.where(place == idx_ref[pl.ds(k, 1), :], 1.0, 0.0).astype(jnp.bfloat16)
        got = jnp.dot(table, hot, preferred_element_type=jnp.float32)
        equiv = got[:members]
        facts = (
            got[members : members + extra]
            + got[members + extra : members + 2 * extra]
            + got[members + 2 * extra : members + 3 * extra]
        )
        mean = jnp.sum(equiv, axis=0, keepdims=True) * (1.0 / members)
        dist = (facts[2:3] - row_ref[...]) ** 2 + (facts[3:4] - col_ref[...]) ** 2
        rho = jnp.exp(-dist / (2.0 * radius * radius)) / facts[1:2]
        scale = jnp.sqrt(jnp.where(k < cnt_ref[...], rho, 0.0))
        scaled = (equiv - mean) * scale
        dev_ref[pl.ds(k, members, stride=slots), :] = scaled
        innov[pl.ds(k, 1), :] = (facts[0:1] - mean) * scale
        return total + jnp.sum(scaled * scaled, axis=0, keepdims=True)

    spread = lax.fori_loop(0, slots, pick, jnp.zeros((1, LANES), jnp.float32))
    shift = members - 1.0
    trace = spread + shift * members
    inverse = 1.0 / trace
    level = lax.broadcasted_iota(jnp.int32, (slots, LANES), 0)

    def eye(i, value):
        return jnp.where(level == i, value, 0.0)

    def at(ref, k):
        return ref[pl.ds(k * slots if isinstance(k, int) else pl.multiple_of(k * slots, slots), slots), :]

    def bcast(ref, index):
        return ref[pl.ds(index, 1), :]

    def put(ref, i, value):
        ref[pl.ds(pl.multiple_of(i * slots, slots), slots), :] = value

    def sym(ref):
        return lambda k, first, r: bcast(ref, k * slots + first + r)

    def start(first, sums):
        for r in range(GROUP):
            put(gram, first + r, sums[r])
            put(prod, first + r, (sums[r] + eye(first + r, shift)) * inverse)
            put(root, first + r, eye(first + r, 1.0))
            put(core, first + r, jnp.zeros((slots, LANES), jnp.float32))

    lane_product(sym(dev_ref), lambda k: at(dev_ref, k), members, slots, slots, start)

    def newton(_, carry):
        p_one, z_one = carry
        m_one = 1.5 - 0.5 * z_one * p_one
        z_next = z_one * m_one
        p_next = p_one * m_one

        def to_half(first, sums):
            for r in range(GROUP):
                quot = (shift * at(core, first + r) + at(root, first + r)) * inverse
                put(half, first + r, -0.5 * (sums[r] + z_one * quot))

        lane_product(sym(core), lambda k: at(prod, k), slots, slots, slots, to_half)

        def to_core(first, sums):
            for r in range(GROUP):
                put(core, first + r, m_one * at(core, first + r) + sums[r])

        lane_product(sym(half), lambda k: at(root, k), slots, slots, slots, to_core)

        def to_root(first, sums):
            for r in range(GROUP):
                put(root, first + r, sums[r] + eye(first + r, z_next))

        lane_product(sym(gram), lambda k: at(core, k), slots, slots, slots, to_root)

        def to_prod(first, sums):
            for r in range(GROUP):
                put(prod, first + r, (sums[r] + shift * at(root, first + r)) * inverse)

        lane_product(sym(gram), lambda k: at(root, k), slots, slots, slots, to_prod)
        return p_next, z_next

    one = jnp.ones((1, LANES), jnp.float32)
    _, z_last = lax.fori_loop(0, repeats, newton, (shift * inverse, one))

    def apply_root(k, total):
        return total + bcast(innov, k) * at(root, k)

    none = jnp.zeros((slots, LANES), jnp.float32)
    innov[...] = lax.fori_loop(0, slots, apply_root, none)
    gain = lax.fori_loop(0, slots, apply_root, none) * inverse
    factor = math.sqrt(shift) * jnp.sqrt(inverse)
    keep_ref[...] = factor * z_last

    def to_mix(first, sums):
        for r in range(GROUP):
            put(mix_ref, first + r, factor * sums[r] + gain)

    lane_product(
        lambda k, first, r: bcast(dev_ref, (first + r) * slots + k),
        lambda k: at(core, k), slots, members, slots, to_mix,
    )


def solve_cells(pool, idx, counts, rows, cols, members):
    slots, cells = idx.shape
    lane = lambda height: pl.BlockSpec((height, LANES), lambda c: (0, c))
    square = pltpu.VMEM((slots * slots, LANES), jnp.float32)
    return pl.pallas_call(
        functools.partial(weights_kernel, members, NEWTON, LOC),
        grid=(cells // LANES,),
        in_specs=[pl.BlockSpec(pool.shape, lambda c: (0, 0)), lane(slots), lane(1), lane(1), lane(1)],
        out_specs=[lane(members * slots), lane(members * slots), lane(1)],
        out_shape=[
            jax.ShapeDtypeStruct((members * slots, cells), jnp.float32),
            jax.ShapeDtypeStruct((members * slots, cells), jnp.float32),
            jax.ShapeDtypeStruct((1, cells), jnp.float32),
        ],
        scratch_shapes=[square] * 5 + [pltpu.VMEM((slots, LANES), jnp.float32)],
        compiler_params=pltpu.CompilerParams(vmem_limit_bytes=40 * 1024 * 1024),
        cost_estimate=pl.CostEstimate(flops=2 * 10**9, bytes_accessed=200 * 10**6, transcendentals=0),
        interpret=INTERPRET,
    )(pool, idx, counts, rows, cols)


def analysis_kernel(parts, slots, *refs):
    states = refs[:parts]
    dev_ref, mix_ref, keep_ref = refs[parts : parts + 3]
    outs = refs[parts + 3 : 2 * parts + 3]
    anomaly, mapped, mean_ref = refs[2 * parts + 3 :]
    share, width, _ = states[0].shape
    members = share * parts
    total = jnp.zeros((width, LANES), jnp.float32)
    for state in states:
        total = lax.fori_loop(
            0, share, lambda i, t, s=state: t + s[i].astype(jnp.float32), total, unroll=4
        )
    mean = total * (1.0 / members)
    mean_ref[...] = mean
    for part, state in enumerate(states):

        def subtract(i, carry, s=state, base=part * share):
            anomaly[base + i] = s[i].astype(jnp.float32) - mean_ref[...]
            return carry

        lax.fori_loop(0, share, subtract, 0, unroll=4)

    def to_mapped(first, sums):
        for r in range(GROUP):
            mapped[first + r] = sums[r]

    lane_product(
        lambda i, first, r: dev_ref[pl.ds(i * slots + first + r, 1), :],
        lambda i: anomaly[i], members, slots, width, to_mapped,
    )
    for part, out in enumerate(outs):
        base = part * share

        def to_out(first, sums, out=out, base=base):
            for r in range(GROUP):
                held = mean_ref[...] + keep_ref[...] * anomaly[base + first + r]
                out[first + r] = (held + sums[r]).astype(jnp.bfloat16)

        lane_product(
            lambda k, first, r, base=base: mix_ref[pl.ds((base + first + r) * slots + k, 1), :],
            lambda k: mapped[k], slots, share, width, to_out,
        )


def analyse(states, dev, mix, keep, slots, first, count, width):
    share, _, cells = states[0].shape
    parts = len(states)
    members = share * parts
    wide = lambda height: pl.BlockSpec((height, LANES), lambda c, f: (0, c))
    return pl.pallas_call(
        functools.partial(analysis_kernel, parts, slots),
        grid=(cells // LANES, count // width),
        in_specs=[
            pl.BlockSpec((share, width, LANES), lambda c, f: (0, f + first // width, c))
        ] * parts + [wide(members * slots), wide(members * slots), wide(1)],
        out_specs=[pl.BlockSpec((share, width, LANES), lambda c, f: (0, f, c))] * parts,
        out_shape=[jax.ShapeDtypeStruct((share, count, cells), jnp.bfloat16)] * parts,
        scratch_shapes=[
            pltpu.VMEM((members, width, LANES), jnp.float32),
            pltpu.VMEM((slots, width, LANES), jnp.float32),
            pltpu.VMEM((width, LANES), jnp.float32),
        ],
        compiler_params=pltpu.CompilerParams(vmem_limit_bytes=32 * 1024 * 1024),
        cost_estimate=pl.CostEstimate(flops=10**9, bytes_accessed=50 * 10**6, transcendentals=0),
        interpret=INTERPRET,
    )(*states, dev, mix, keep)


def halo(cells, width):
    count = lax.axis_size("space")
    before = lax.ppermute(cells[-width:], "space", [(i, i + 1) for i in range(count - 1)])
    after = lax.ppermute(cells[:width], "space", [(i + 1, i) for i in range(count - 1)])
    return before, after


def wide_rows(cells, width):
    before, after = halo(cells, width)
    return jnp.concatenate([before, cells, after], axis=0)


def row_step(south, middle, north, courant):
    return (
        middle
        - 0.5 * courant * (north - south)
        + 0.5 * courant * courant * (north - 2.0 * middle + south)
    )


def col_step(middle, courant):
    padded = jnp.pad(middle, [(0, 0)] * (middle.ndim - 1) + [(1, 1)])
    east, west = padded[..., 2:], padded[..., :-2]
    return (
        middle
        - 0.5 * courant * (east - west)
        + 0.5 * courant * courant * (east - 2.0 * middle + west)
    )


def shards(
    ensemble, obs_value, obs_error, obs_cell, obs_species, patch_index, patch_count,
    courant_x, courant_y, dep_velocity, surface_factor,
):
    local_members, fields, tile_rows, columns = ensemble.shape
    species = dep_velocity.shape[0]
    levels = fields // species
    tile_cells = tile_rows * columns
    groups = lax.axis_size("mem")
    members = local_members * groups
    me = lax.axis_index("mem")
    slots = patch_index.shape[2]
    per_dev = tile_cells // groups
    paired = groups == 2 and tile_rows == 2 and columns % LANES == 0
    swap = [(0, 1), (1, 0)]

    if paired:
        mine = lax.dynamic_index_in_dim(ensemble, me, 2, keepdims=False)
        theirs = lax.dynamic_index_in_dim(ensemble, 1 - me, 2, keepdims=False)
    surface = ensemble.reshape(local_members, species, levels, tile_cells)[:, :, 0]
    position = obs_species[0] * tile_cells + obs_cell[0]
    equiv = jnp.take(surface.reshape(local_members, -1), position, axis=1).astype(jnp.float32)
    if paired:
        equiv = jnp.concatenate([equiv, lax.ppermute(equiv, "mem", swap)], axis=0)
    else:
        equiv = lax.all_gather(equiv, "mem", axis=0, tiled=True)
    zeros = jnp.zeros_like(obs_value[0])
    info = jnp.stack(
        [
            obs_value[0],
            obs_error[0],
            (obs_cell[0] // columns).astype(jnp.float32),
            (obs_cell[0] % columns).astype(jnp.float32),
        ]
        + [zeros] * 4
    )
    packed = jnp.concatenate([equiv, info], axis=0)
    before, after = halo(packed[None], 1)
    offset = jnp.zeros((packed.shape[0], 1), jnp.float32).at[members + 2, 0].set(float(tile_rows))
    pool = jnp.concatenate([before[0] - offset, packed, after[0] + offset], axis=1)

    if paired:
        states = (mine, lax.ppermute(theirs, "mem", swap))
    else:
        states = (
            lax.all_to_all(
                ensemble.reshape(local_members, fields, tile_cells),
                "mem", split_axis=2, concat_axis=0, tiled=True,
            ),
        )
    spare = -per_dev % LANES
    pad = lambda a: jnp.pad(a, [(0, 0)] * (a.ndim - 1) + [(0, spare)]) if spare else a
    states = tuple(pad(state) for state in states)
    cell = me * per_dev + jnp.arange(per_dev, dtype=jnp.int32)
    dev, mix, keep = solve_cells(
        pool,
        pad(jnp.transpose(patch_index[0])),
        pad(patch_count),
        pad((cell // columns).astype(jnp.float32)[None]),
        pad((cell % columns).astype(jnp.float32)[None]),
        members,
    )

    width = next(w for w in (32, 16, fields) if fields % w == 0)
    blocks = fields // width
    parts = 2 if paired and blocks > 1 and width % levels == 0 else 1
    cuts = [0, (blocks + 1) // 2 * width, fields] if parts == 2 else [0, fields]
    wide_x = wide_rows(jnp.moveaxis(courant_x, 1, 0), SUBSTEPS)
    wide_y = wide_rows(jnp.moveaxis(courant_y, 1, 0), SUBSTEPS)
    loss = jnp.exp(-dep_velocity[:, None, None] * surface_factor[None])

    results = []
    for low, high in zip(cuts[:-1], cuts[1:]):
        count = high - low
        out = analyse(states, dev, mix, keep, slots, low, count, width)
        if paired:
            other = lax.ppermute(out[1], "mem", swap)
            rows = jnp.stack([jnp.where(me == 0, out[0], other), jnp.where(me == 0, other, out[0])])
        else:
            back = lax.all_to_all(out[0][..., :per_dev], "mem", split_axis=0, concat_axis=2, tiled=True)
            rows = jnp.moveaxis(back.reshape(local_members, count, tile_rows, columns), 2, 0)
        south, north = halo(rows, SUBSTEPS)
        shape = (local_members, count // levels, levels, columns)
        now = [
            part[r].reshape(shape).astype(jnp.float32)
            for part in (south, rows, north)
            for r in range(part.shape[0])
        ]
        for repeat in range(SUBSTEPS):
            first = repeat + 1
            now = [
                col_step(
                    row_step(now[r - 1], now[r], now[r + 1], wide_y[first + r - 1]),
                    wide_x[first + r - 1],
                )
                for r in range(1, len(now) - 1)
            ]
        part = loss[low // levels : high // levels]
        lowest = (jnp.arange(levels, dtype=jnp.int32) == 0)[:, None]
        now = [
            row * jnp.where(lowest, part[:, r][:, None], 1.0) for r, row in enumerate(now)
        ]
        joined = jnp.stack([row.astype(jnp.bfloat16) for row in now], axis=3)
        results.append(joined.reshape(local_members, count, tile_rows, columns))
    return jnp.concatenate(results, axis=1) if len(results) > 1 else results[0]


def solution(mesh):
    in_specs = (
        P("mem", None, "space", None),
        P("space", None),
        P("space", None),
        P("space", None),
        P("space", None),
        P("space", "mem", None),
        P("space", "mem"),
        P(None, "space", None),
        P(None, "space", None),
        P(),
        P("space", None),
    )
    out_specs = P("mem", None, "space", None)
    return jax.shard_map(shards, mesh=mesh, in_specs=in_specs, out_specs=out_specs, check_vma=False)
```

```python
import functools
import math

import jax
import jax.numpy as jnp
from jax import lax
from jax.experimental import pallas as pl
from jax.experimental.pallas import tpu as pltpu
from jax.sharding import PartitionSpec as P

NEWTON = 8
SUBSTEPS = 2
LOC = 1
LANES = 128
GROUP = 8
INTERPRET = False


def lane_product(left, right, depth, rows, width, finish, unroll=4):
    def group(block, carry):
        first = pl.multiple_of(block * GROUP, GROUP)

        def step(k, sums):
            row = right(k)
            return tuple(sums[r] + left(k, first, r) * row for r in range(GROUP))

        zero = jnp.zeros((width, LANES), jnp.float32)
        sums = lax.fori_loop(0, depth, step, (zero,) * GROUP, unroll=unroll)
        finish(first, sums)
        return carry

    lax.fori_loop(0, rows // GROUP, group, 0)


def weights_kernel(
    members, repeats, radius,
    pool_ref, idx_ref, cnt_ref, row_ref, col_ref,
    dev_ref, mix_ref, keep_ref,
    gram, prod, root, core, half, innov,
):
    slots = idx_ref.shape[0]
    pooled = pool_ref.shape[1]
    info = pool_ref[members:, :]
    high = info.astype(jnp.bfloat16).astype(jnp.float32)
    rest = info - high
    middle = rest.astype(jnp.bfloat16).astype(jnp.float32)
    low = rest - middle
    table = jnp.concatenate([pool_ref[:members, :], high, middle, low, jnp.zeros_like(low)], axis=0)
    table = table.astype(jnp.bfloat16)
    place = lax.broadcasted_iota(jnp.int32, (pooled, LANES), 0)
    extra = info.shape[0]

    def pick(k, total):
        hot = jnp.where(place == idx_ref[pl.ds(k, 1), :], 1.0, 0.0).astype(jnp.bfloat16)
        got = jnp.dot(table, hot, preferred_element_type=jnp.float32)
        equiv = got[:members]
        facts = (
            got[members : members + extra]
            + got[members + extra : members + 2 * extra]
            + got[members + 2 * extra : members + 3 * extra]
        )
        mean = jnp.sum(equiv, axis=0, keepdims=True) * (1.0 / members)
        dist = (facts[2:3] - row_ref[...]) ** 2 + (facts[3:4] - col_ref[...]) ** 2
        rho = jnp.exp(-dist / (2.0 * radius * radius)) / facts[1:2]
        scale = jnp.sqrt(jnp.where(k < cnt_ref[...], rho, 0.0))
        scaled = (equiv - mean) * scale
        dev_ref[pl.ds(k, members, stride=slots), :] = scaled
        innov[pl.ds(k, 1), :] = (facts[0:1] - mean) * scale
        return total + jnp.sum(scaled * scaled, axis=0, keepdims=True)

    spread = lax.fori_loop(0, slots, pick, jnp.zeros((1, LANES), jnp.float32))
    shift = members - 1.0
    trace = spread + shift * members
    inverse = 1.0 / trace
    level = lax.broadcasted_iota(jnp.int32, (slots, LANES), 0)

    def eye(i, value):
        return jnp.where(level == i, value, 0.0)

    def at(ref, k):
        return ref[pl.ds(k * slots if isinstance(k, int) else pl.multiple_of(k * slots, slots), slots), :]

    def bcast(ref, index):
        return ref[pl.ds(index, 1), :]

    def put(ref, i, value):
        ref[pl.ds(pl.multiple_of(i * slots, slots), slots), :] = value

    def sym(ref):
        return lambda k, first, r: bcast(ref, k * slots + first + r)

    def start(first, sums):
        for r in range(GROUP):
            put(gram, first + r, sums[r])
            put(prod, first + r, (sums[r] + eye(first + r, shift)) * inverse)
            put(root, first + r, eye(first + r, 1.0))
            put(core, first + r, jnp.zeros((slots, LANES), jnp.float32))

    lane_product(sym(dev_ref), lambda k: at(dev_ref, k), members, slots, slots, start)

    def newton(_, carry):
        p_one, z_one = carry
        m_one = 1.5 - 0.5 * z_one * p_one
        z_next = z_one * m_one
        p_next = p_one * m_one

        def to_half(first, sums):
            for r in range(GROUP):
                quot = (shift * at(core, first + r) + at(root, first + r)) * inverse
                put(half, first + r, -0.5 * (sums[r] + z_one * quot))

        lane_product(sym(core), lambda k: at(prod, k), slots, slots, slots, to_half)

        def to_core(first, sums):
            for r in range(GROUP):
                put(core, first + r, m_one * at(core, first + r) + sums[r])

        lane_product(sym(half), lambda k: at(root, k), slots, slots, slots, to_core)

        def to_root(first, sums):
            for r in range(GROUP):
                put(root, first + r, sums[r] + eye(first + r, z_next))

        lane_product(sym(gram), lambda k: at(core, k), slots, slots, slots, to_root)

        def to_prod(first, sums):
            for r in range(GROUP):
                put(prod, first + r, (sums[r] + shift * at(root, first + r)) * inverse)

        lane_product(sym(gram), lambda k: at(root, k), slots, slots, slots, to_prod)
        return p_next, z_next

    one = jnp.ones((1, LANES), jnp.float32)
    _, z_last = lax.fori_loop(0, repeats, newton, (shift * inverse, one))

    def apply_root(k, total):
        return total + bcast(innov, k) * at(root, k)

    none = jnp.zeros((slots, LANES), jnp.float32)
    innov[...] = lax.fori_loop(0, slots, apply_root, none)
    gain = lax.fori_loop(0, slots, apply_root, none) * inverse
    factor = math.sqrt(shift) * jnp.sqrt(inverse)
    keep_ref[...] = factor * z_last

    def to_mix(first, sums):
        for r in range(GROUP):
            put(mix_ref, first + r, factor * sums[r] + gain)

    lane_product(
        lambda k, first, r: bcast(dev_ref, (first + r) * slots + k),
        lambda k: at(core, k), slots, members, slots, to_mix,
    )


def solve_cells(pool, idx, counts, rows, cols, members):
    slots, cells = idx.shape
    lane = lambda height: pl.BlockSpec((height, LANES), lambda c: (0, c))
    square = pltpu.VMEM((slots * slots, LANES), jnp.float32)
    return pl.pallas_call(
        functools.partial(weights_kernel, members, NEWTON, LOC),
        grid=(cells // LANES,),
        in_specs=[pl.BlockSpec(pool.shape, lambda c: (0, 0)), lane(slots), lane(1), lane(1), lane(1)],
        out_specs=[lane(members * slots), lane(members * slots), lane(1)],
        out_shape=[
            jax.ShapeDtypeStruct((members * slots, cells), jnp.float32),
            jax.ShapeDtypeStruct((members * slots, cells), jnp.float32),
            jax.ShapeDtypeStruct((1, cells), jnp.float32),
        ],
        scratch_shapes=[square] * 5 + [pltpu.VMEM((slots, LANES), jnp.float32)],
        compiler_params=pltpu.CompilerParams(vmem_limit_bytes=40 * 1024 * 1024),
        cost_estimate=pl.CostEstimate(flops=2 * 10**9, bytes_accessed=200 * 10**6, transcendentals=0),
        interpret=INTERPRET,
    )(pool, idx, counts, rows, cols)


def analysis_kernel(parts, slots, *refs):
    states = refs[:parts]
    dev_ref, mix_ref, keep_ref = refs[parts : parts + 3]
    outs = refs[parts + 3 : 2 * parts + 3]
    anomaly, mapped, mean_ref = refs[2 * parts + 3 :]
    share, width, _ = states[0].shape
    members = share * parts
    total = jnp.zeros((width, LANES), jnp.float32)
    for state in states:
        total = lax.fori_loop(
            0, share, lambda i, t, s=state: t + s[i].astype(jnp.float32), total, unroll=4
        )
    mean = total * (1.0 / members)
    mean_ref[...] = mean
    for part, state in enumerate(states):

        def subtract(i, carry, s=state, base=part * share):
            anomaly[base + i] = s[i].astype(jnp.float32) - mean_ref[...]
            return carry

        lax.fori_loop(0, share, subtract, 0, unroll=4)

    def to_mapped(first, sums):
        for r in range(GROUP):
            mapped[first + r] = sums[r]

    lane_product(
        lambda i, first, r: dev_ref[pl.ds(i * slots + first + r, 1), :],
        lambda i: anomaly[i], members, slots, width, to_mapped,
    )
    for part, out in enumerate(outs):
        base = part * share

        def to_out(first, sums, out=out, base=base):
            for r in range(GROUP):
                held = mean_ref[...] + keep_ref[...] * anomaly[base + first + r]
                out[first + r] = (held + sums[r]).astype(jnp.bfloat16)

        lane_product(
            lambda k, first, r, base=base: mix_ref[pl.ds((base + first + r) * slots + k, 1), :],
            lambda k: mapped[k], slots, share, width, to_out,
        )


def analyse(states, dev, mix, keep, slots, first, count, width):
    share, _, cells = states[0].shape
    parts = len(states)
    members = share * parts
    wide = lambda height: pl.BlockSpec((height, LANES), lambda c, f: (0, c))
    return pl.pallas_call(
        functools.partial(analysis_kernel, parts, slots),
        grid=(cells // LANES, count // width),
        in_specs=[
            pl.BlockSpec((share, width, LANES), lambda c, f: (0, f + first // width, c))
        ] * parts + [wide(members * slots), wide(members * slots), wide(1)],
        out_specs=[pl.BlockSpec((share, width, LANES), lambda c, f: (0, f, c))] * parts,
        out_shape=[jax.ShapeDtypeStruct((share, count, cells), jnp.bfloat16)] * parts,
        scratch_shapes=[
            pltpu.VMEM((members, width, LANES), jnp.float32),
            pltpu.VMEM((slots, width, LANES), jnp.float32),
            pltpu.VMEM((width, LANES), jnp.float32),
        ],
        compiler_params=pltpu.CompilerParams(vmem_limit_bytes=32 * 1024 * 1024),
        cost_estimate=pl.CostEstimate(flops=10**9, bytes_accessed=50 * 10**6, transcendentals=0),
        interpret=INTERPRET,
    )(*states, dev, mix, keep)


def halo(cells, width):
    count = lax.axis_size("space")
    before = lax.ppermute(cells[-width:], "space", [(i, i + 1) for i in range(count - 1)])
    after = lax.ppermute(cells[:width], "space", [(i + 1, i) for i in range(count - 1)])
    return before, after


def wide_rows(cells, width):
    before, after = halo(cells, width)
    return jnp.concatenate([before, cells, after], axis=0)


def row_step(south, middle, north, courant):
    return (
        middle
        - 0.5 * courant * (north - south)
        + 0.5 * courant * courant * (north - 2.0 * middle + south)
    )


def col_step(middle, courant):
    padded = jnp.pad(middle, [(0, 0)] * (middle.ndim - 1) + [(1, 1)])
    east, west = padded[..., 2:], padded[..., :-2]
    return (
        middle
        - 0.5 * courant * (east - west)
        + 0.5 * courant * courant * (east - 2.0 * middle + west)
    )


def shards(
    ensemble, obs_value, obs_error, obs_cell, obs_species, patch_index, patch_count,
    courant_x, courant_y, dep_velocity, surface_factor,
):
    local_members, fields, tile_rows, columns = ensemble.shape
    species = dep_velocity.shape[0]
    levels = fields // species
    tile_cells = tile_rows * columns
    groups = lax.axis_size("mem")
    members = local_members * groups
    me = lax.axis_index("mem")
    slots = patch_index.shape[2]
    per_dev = tile_cells // groups
    paired = groups == 2 and tile_rows == 2 and columns % LANES == 0
    swap = [(0, 1), (1, 0)]

    if paired:
        mine = lax.dynamic_index_in_dim(ensemble, me, 2, keepdims=False)
        theirs = lax.dynamic_index_in_dim(ensemble, 1 - me, 2, keepdims=False)
    surface = ensemble.reshape(local_members, species, levels, tile_cells)[:, :, 0]
    position = obs_species[0] * tile_cells + obs_cell[0]
    equiv = jnp.take(surface.reshape(local_members, -1), position, axis=1).astype(jnp.float32)
    if paired:
        equiv = jnp.concatenate([equiv, lax.ppermute(equiv, "mem", swap)], axis=0)
    else:
        equiv = lax.all_gather(equiv, "mem", axis=0, tiled=True)
    zeros = jnp.zeros_like(obs_value[0])
    info = jnp.stack(
        [
            obs_value[0],
            obs_error[0],
            (obs_cell[0] // columns).astype(jnp.float32),
            (obs_cell[0] % columns).astype(jnp.float32),
        ]
        + [zeros] * 4
    )
    packed = jnp.concatenate([equiv, info], axis=0)
    height = packed.shape[0]
    joint = tile_rows == SUBSTEPS and tile_cells == packed.shape[1]
    if joint:
        courants = jnp.concatenate([courant_x, courant_y]).reshape(2 * levels, tile_cells)
        packed = jnp.concatenate([packed, courants], axis=0)
    before, after = halo(packed[None], 1)
    if joint:
        wide = jnp.concatenate(
            [
                jnp.moveaxis(part[height:].reshape(2, levels, tile_rows, columns), 2, 0)
                for part in (before[0], packed, after[0])
            ]
        )
        wide_x, wide_y = wide[:, 0], wide[:, 1]
        before, packed, after = before[:, :height], packed[:height], after[:, :height]
    else:
        wide_x = wide_rows(jnp.moveaxis(courant_x, 1, 0), SUBSTEPS)
        wide_y = wide_rows(jnp.moveaxis(courant_y, 1, 0), SUBSTEPS)
    offset = jnp.zeros((packed.shape[0], 1), jnp.float32).at[members + 2, 0].set(float(tile_rows))
    pool = jnp.concatenate([before[0] - offset, packed, after[0] + offset], axis=1)

    if paired:
        states = (mine, lax.ppermute(theirs, "mem", swap))
    else:
        states = (
            lax.all_to_all(
                ensemble.reshape(local_members, fields, tile_cells),
                "mem", split_axis=2, concat_axis=0, tiled=True,
            ),
        )
    spare = -per_dev % LANES
    pad = lambda a: jnp.pad(a, [(0, 0)] * (a.ndim - 1) + [(0, spare)]) if spare else a
    states = tuple(pad(state) for state in states)
    cell = me * per_dev + jnp.arange(per_dev, dtype=jnp.int32)
    dev, mix, keep = solve_cells(
        pool,
        pad(jnp.transpose(patch_index[0])),
        pad(patch_count),
        pad((cell // columns).astype(jnp.float32)[None]),
        pad((cell % columns).astype(jnp.float32)[None]),
        members,
    )

    width = next(w for w in (32, 16, fields) if fields % w == 0)
    blocks = fields // width
    step = 2 * width if paired and width % levels == 0 else fields
    cuts = list(range(0, fields, step)) + [fields]
    loss = jnp.exp(-dep_velocity[:, None, None] * surface_factor[None])

    results = []
    for low, high in zip(cuts[:-1], cuts[1:]):
        count = high - low
        out = analyse(states, dev, mix, keep, slots, low, count, width)
        if paired:
            *out, keep = lax.optimization_barrier((*out, keep))
            other = lax.ppermute(out[1], "mem", swap)
            rows = jnp.stack([jnp.where(me == 0, out[0], other), jnp.where(me == 0, other, out[0])])
        else:
            back = lax.all_to_all(out[0][..., :per_dev], "mem", split_axis=0, concat_axis=2, tiled=True)
            rows = jnp.moveaxis(back.reshape(local_members, count, tile_rows, columns), 2, 0)
        south, north = halo(rows, SUBSTEPS)
        shape = (local_members, count // levels, levels, columns)
        now = [
            part[r].reshape(shape).astype(jnp.float32)
            for part in (south, rows, north)
            for r in range(part.shape[0])
        ]
        for repeat in range(SUBSTEPS):
            first = repeat + 1
            now = [
                col_step(
                    row_step(now[r - 1], now[r], now[r + 1], wide_y[first + r - 1]),
                    wide_x[first + r - 1],
                )
                for r in range(1, len(now) - 1)
            ]
        part = loss[low // levels : high // levels]
        lowest = (jnp.arange(levels, dtype=jnp.int32) == 0)[:, None]
        now = [
            row * jnp.where(lowest, part[:, r][:, None], 1.0) for r, row in enumerate(now)
        ]
        joined = jnp.stack([row.astype(jnp.bfloat16) for row in now], axis=3)
        results.append(joined.reshape(local_members, count, tile_rows, columns))
    return jnp.concatenate(results, axis=1) if len(results) > 1 else results[0]


def solution(mesh):
    in_specs = (
        P("mem", None, "space", None),
        P("space", None),
        P("space", None),
        P("space", None),
        P("space", None),
        P("space", "mem", None),
        P("space", "mem"),
        P(None, "space", None),
        P(None, "space", None),
        P(),
        P("space", None),
    )
    out_specs = P("mem", None, "space", None)
    return jax.shard_map(shards, mesh=mesh, in_specs=in_specs, out_specs=out_specs, check_vma=False)
```
